128 devices in a mesh: row: 16 (over y, x), col: 8 (over z, core).
Axes of the slice: x: 4, y: 4, z: 4, core: 2. Of those that a mesh axis runs over, the one named last changes fastest.
Arguments:
- tokens: bfloat16 [1024, 8192], P('col', 'row'), may hold values from -6 to 6
- cotangent: bfloat16 [1024, 8192], P('col', 'row'), may hold values from -1.5 to 1.5
- gate_weight: bfloat16 [8192, 14336], P('row', 'col'), may hold values from -0.0625 to 0.0625
- up_weight: bfloat16 [8192, 14336], P('row', 'col'), may hold values from -0.0625 to 0.0625
- down_weight: bfloat16 [14336, 8192], P('col', 'row'), may hold values from -0.046875 to 0.046875
Outputs:
- layer_output: bfloat16 [1024, 8192], P('col', 'row')
- input_grad: bfloat16 [1024, 8192], P('col', 'row')
- gate_weight_grad: bfloat16 [8192, 14336], P('row', 'col')
- up_weight_grad: bfloat16 [8192, 14336], P('row', 'col')
- down_weight_grad: bfloat16 [14336, 8192], P('col', 'row')
The draws below stay inside these ranges and needn't reach their ends.
All inputs are finite; a program needn't handle non-finite values.
Results may differ from the reference program's by a relative error of at most 0.0049.
Values may be sent and summed in bfloat16 or wider, within the bound.
No kernel may reach another device: no remote copies, remote signals or barrier semaphores. Data moves between devices by JAX's collectives and lax.ppermute only.
A program may use at most 192 MiB of HBM per device.

```python
import jax
import jax.numpy as jnp

D = 8192
FF = 14336
TOKENS = 1024


def levels(stream_key, extent, split, least, top_value):
    level = 1.0
    for dim, parts in split:
        draws = jax.random.uniform(jax.random.fold_in(jax.random.fold_in(stream_key, 6), dim), (parts,), jnp.float32, least / len(split), top_value / len(split))
        level = level * jnp.repeat(jnp.exp(draws), extent[dim] // parts).reshape((-1,) + (1,) * (len(extent) - 1 - dim))
    return level


def centred(own_key, dims, deviation, bound, shards=(), held_as=jnp.bfloat16):
    factor_of = levels(own_key, dims, shards, -0.22, 0.18) if shards else 1.0
    values = jax.random.normal(own_key, dims, jnp.float32) * deviation * factor_of
    return jnp.minimum(jnp.maximum(values, -bound), bound).astype(held_as)


def setup_inputs(seed: int = 0) -> dict:
    key_of = jax.random.split(jax.random.key(seed), 6)
    tokens = centred(key_of[0], (TOKENS, D), 1.0, 6.0, ((0, 8), (1, 16)))
    cotangent = centred(key_of[1], (TOKENS, D), 0.25, 1.5, ((0, 8), (1, 16)))
    gate_weight = centred(key_of[2], (D, FF), D ** -0.5, 0.0625, ((0, 16), (1, 8)))
    up_weight = centred(key_of[3], (D, FF), D ** -0.5, 0.0625, ((0, 16), (1, 8)))
    down_weight = centred(key_of[4], (FF, D), FF ** -0.5, 0.046875, ((0, 8), (1, 16)))
    return dict(tokens=tokens, cotangent=cotangent, gate_weight=gate_weight, up_weight=up_weight, down_weight=down_weight)


def reference(tokens, cotangent, gate_weight, up_weight, down_weight):
    gate_sum = jnp.dot(tokens, gate_weight, preferred_element_type=jnp.float32)
    up_sum = jnp.dot(tokens, up_weight, preferred_element_type=jnp.float32)
    sigmoid_gate = jax.nn.sigmoid(gate_sum)
    silu_gate = gate_sum * sigmoid_gate
    hidden = (silu_gate * up_sum).astype(jnp.bfloat16)
    layer_output = jnp.dot(hidden, down_weight, preferred_element_type=jnp.float32).astype(jnp.bfloat16)
    hidden_grad = jnp.dot(cotangent, down_weight.T, preferred_element_type=jnp.float32)
    down_weight_grad = jnp.dot(hidden.T, cotangent, preferred_element_type=jnp.float32).astype(jnp.bfloat16)
    silu_slope = sigmoid_gate * (1.0 + gate_sum * (1.0 - sigmoid_gate))
    gate_grad = (hidden_grad * up_sum * silu_slope).astype(jnp.bfloat16)
    up_grad = (hidden_grad * silu_gate).astype(jnp.bfloat16)
    input_sum = jnp.dot(gate_grad, gate_weight.T, preferred_element_type=jnp.float32) + jnp.dot(up_grad, up_weight.T, preferred_element_type=jnp.float32)
    input_grad = input_sum.astype(jnp.bfloat16)
    gate_weight_grad = jnp.dot(tokens.T, gate_grad, preferred_element_type=jnp.float32).astype(jnp.bfloat16)
    up_weight_grad = jnp.dot(tokens.T, up_grad, preferred_element_type=jnp.float32).astype(jnp.bfloat16)
    return (layer_output, input_grad, gate_weight_grad, up_weight_grad, down_weight_grad)
```

```python
import jax
import jax.numpy as jnp
from jax import lax
from jax.experimental import pallas as pl
from jax.experimental.pallas import tpu as pltpu
from jax.sharding import PartitionSpec as P

F32, BF16 = jnp.float32, jnp.bfloat16


def contract_last(left, right):
    return lax.dot_general(left, right, (((1,), (1,)), ((), ())), preferred_element_type=F32)


def contract_first(left, right):
    return lax.dot_general(left, right, (((0,), (0,)), ((), ())), preferred_element_type=F32)


def shift(value, axis, step):
    if axis == "x":
        name, pairs = "row", [(y * 4 + x, y * 4 + (x + step) % 4) for y in range(4) for x in range(4)]
    elif axis == "y":
        name, pairs = "row", [(y * 4 + x, (y + step) % 4 * 4 + x) for y in range(4) for x in range(4)]
    elif axis == "z":
        name, pairs = "col", [(z * 2 + c, (z + step) % 4 * 2 + c) for z in range(4) for c in range(2)]
    else:
        name, pairs = "col", [(z * 2 + c, z * 2 + 1 - c) for z in range(4) for c in range(2)]
    return lax.ppermute(value, name, pairs)


def reorder(source, value):
    blocks = value.reshape(32, 32, value.shape[-1])

    def kernel(source_ref, in_ref, out_ref):
        for block in range(32):
            out_ref[block] = in_ref[source_ref[block]]

    return pl.pallas_call(
        kernel,
        out_shape=jax.ShapeDtypeStruct(blocks.shape, blocks.dtype),
        in_specs=[pl.BlockSpec(memory_space=pltpu.SMEM), pl.BlockSpec(memory_space=pltpu.VMEM)],
        out_specs=pl.BlockSpec(memory_space=pltpu.VMEM),
        cost_estimate=pl.CostEstimate(flops=0, bytes_accessed=2 * blocks.size * blocks.dtype.itemsize, transcendentals=0),
    )(source, blocks).reshape(value.shape)


def gather_ring(value, axis):
    return jnp.concatenate([value] + [shift(value, axis, -k) for k in (1, 2, 3)], axis=0)


def gather_ring_relayed(value, axis):
    half = value.shape[0] // 2
    ahead = shift(value, axis, -1)
    behind = shift(value, axis, 1)
    far_top = shift(ahead[:half], axis, -1)
    far_bottom = shift(behind[half:], axis, 1)
    return jnp.concatenate([value, ahead, far_top, far_bottom, behind], axis=0)


def scatter_ring_relayed(chunks, axis, dtype):
    half = chunks[0].shape[0] // 2
    far = chunks[2].astype(dtype)
    from_behind = shift(far[:half], axis, 1)
    from_ahead = shift(far[half:], axis, -1)
    ahead = jnp.concatenate([chunks[1][:half] + from_behind, chunks[1][half:]], axis=0).astype(dtype)
    behind = jnp.concatenate([chunks[3][:half], chunks[3][half:] + from_ahead], axis=0).astype(dtype)
    return chunks[0] + shift(ahead, axis, 1).astype(F32) + shift(behind, axis, -1).astype(F32)


def scatter_ring(chunks, axis, dtype):
    total = chunks[0]
    for k in (1, 2, 3):
        total = total + shift(chunks[k].astype(dtype), axis, k).astype(F32)
    return total


def cut(value, parts):
    rows = value.shape[0] // parts
    return [value[k * rows:(k + 1) * rows] for k in range(parts)]


def scatter_rows(partial):
    upper, lower = cut(partial, 2)
    own = []
    for part, first, second in ((upper, "x", "y"), (lower, "y", "x")):
        summed = scatter_ring_relayed(cut(part, 4), first, BF16)
        own.append(scatter_ring(cut(summed, 4), second, F32))
    return jnp.concatenate(own, axis=0)


def gather_rows(own):
    upper, lower = cut(own, 2)
    upper = gather_ring_relayed(gather_ring(upper, "y"), "x")
    lower = gather_ring_relayed(gather_ring(lower, "x"), "y")
    return jnp.concatenate([upper, lower], axis=0)


def local(tokens, cotangent, gate_weight, up_weight, down_weight):
    row, col = lax.axis_index("row"), lax.axis_index("col")
    x, y, z, core = row % 4, row // 4, col // 2, col % 2
    at = jnp.arange(32, dtype=jnp.int32)
    major, minor = at // 4 % 4, at % 4
    is_lower = at // 16
    block = is_lower * 4 + (major + jnp.where(is_lower == 0, x, y)) % 4
    sub = (minor + jnp.where(is_lower == 0, y, x)) % 4
    to_panel = (block % 2 - core) % 2 * 16 + (block // 2 - z) % 4 * 4 + sub
    block = (z + major) % 4 * 2 + (core + is_lower) % 2
    in_lower = block // 4
    from_panel = in_lower * 16 + (block - jnp.where(in_lower == 0, x, 4 + y)) % 4 * 4 + (minor - jnp.where(in_lower == 0, y, x)) % 4

    def panel_of(value):
        mine = gather_ring(value, "z")
        return reorder(to_panel, jnp.concatenate([mine, shift(mine, "core", 1)], axis=0))

    def scatter_cols(partial):
        mine, other = cut(reorder(from_panel, partial), 2)
        summed = mine + shift(other, "core", 1)
        return scatter_ring(cut(summed, 4), "z", BF16).astype(BF16)

    width = gate_weight.shape[1]
    token_panel = panel_of(tokens)
    grad_panel = panel_of(cotangent)
    gate_up = scatter_rows(
        jnp.concatenate(
            [
                jnp.dot(token_panel, gate_weight, preferred_element_type=F32),
                jnp.dot(token_panel, up_weight, preferred_element_type=F32),
            ],
            axis=1,
        )
    )
    hidden_grad = scatter_rows(contract_last(grad_panel, down_weight))
    gate, up = gate_up[:, :width], gate_up[:, width:]
    sigmoid_gate = jax.nn.sigmoid(gate)
    silu_gate = gate * sigmoid_gate
    hidden = (silu_gate * up).astype(BF16)
    hidden_panel = gather_rows(hidden)
    gate_grad = (hidden_grad * up * (sigmoid_gate * (1.0 + gate * (1.0 - sigmoid_gate)))).astype(BF16)
    up_grad = (hidden_grad * silu_gate).astype(BF16)
    both = gather_rows(jnp.concatenate([gate_grad, up_grad], axis=1))
    gate_grad_panel, up_grad_panel = both[:, :width], both[:, width:]
    layer_output = scatter_cols(jnp.dot(hidden_panel, down_weight, preferred_element_type=F32))
    input_grad = scatter_cols(
        contract_last(gate_grad_panel, gate_weight) + contract_last(up_grad_panel, up_weight)
    )
    down_weight_grad = contract_first(hidden_panel, grad_panel).astype(BF16)
    gate_weight_grad = contract_first(token_panel, gate_grad_panel).astype(BF16)
    up_weight_grad = contract_first(token_panel, up_grad_panel).astype(BF16)
    return (layer_output, input_grad, gate_weight_grad, up_weight_grad, down_weight_grad)


def solution(mesh):
    act, wide = P("col", "row"), P("row", "col")
    return jax.shard_map(
        local,
        mesh=mesh,
        in_specs=(act, act, wide, wide, act),
        out_specs=(act, act, wide, wide, act),
        check_vma=False,
    )
```
